256 devices in a mesh: loop: 32 (over z, x_lo, core), group: 8 (over y, x_hi).
Axes of the slice: x: 4 (x_hi: 2, x_lo: 2; x = x_hi * 2 + x_lo), y: 4, z: 8, core: 2. Of those that a mesh axis runs over, the one named last changes fastest.
Arguments:
- images: bfloat16 [8, 256, 7, 7, 1536], P('group', 'loop'), as said below
- targets: int32 [8, 256], P('group'), may hold values from 0 to 131071, as said below
- kernel: bfloat16 [7, 7, 1536], replicated, may hold values from -0.875 to 0.875
- projection: bfloat16 [1536, 768], replicated, as said below
- captions: bfloat16 [131072, 768], P('loop'), as said below
Outputs:
- loss: float32 [8, 256], P('group', 'loop')
- image_grad: bfloat16 [8, 256, 7, 7, 1536], P('group', 'loop')
- kernel_grad: float32 [1536, 49], P(('loop', 'group'))
The draws below stay inside these ranges and needn't reach their ends.
Inputs may be any that keep to these rules, and one draw needn't show every extreme that they name: targets index captions of the whole gallery. `images`: finite real values. `projection`: finite real values. `captions`: finite real values, no caption all zero.
All inputs are finite; a program needn't handle non-finite values.
Results may differ from the reference program's by a relative error of at most 0.0066.
Values may be sent and summed in bfloat16 or wider, within the bound.
A program may use at most 64 MiB of HBM per device.

```python
import math
import jax
import jax.numpy as jnp
from jax import lax

C = 1536
EMB = 768
KS = 7
SIDE = 7
IMG_DEV = 8
KK = 49
QPG = 256
GROUPS = 8
CAPTIONS = 131072


def cluster_plan(key):
    base_key = jax.random.fold_in(key, 7001)
    cluster_count = 4 * GROUPS
    per_cluster = CAPTIONS // cluster_count
    caption_order = jax.random.permutation(jax.random.fold_in(base_key, 1), CAPTIONS).astype(jnp.int32)
    offsets = jax.random.randint(jax.random.fold_in(base_key, 2), (GROUPS, QPG), 0, 8, dtype=jnp.int32)
    group_ids = lax.broadcasted_iota(jnp.int32, (GROUPS, QPG), 0)
    chosen = (4 * group_ids + offsets) % cluster_count
    ranking = jax.random.randint(jax.random.fold_in(base_key, 3), (GROUPS, QPG), 0, per_cluster, dtype=jnp.int32)
    targets = caption_order[chosen * per_cluster + ranking]
    group_pick = jax.random.randint(jax.random.fold_in(base_key, 4), (), 0, GROUPS, dtype=jnp.int32)
    first_slot = jax.random.randint(jax.random.fold_in(base_key, 5), (), 0, QPG, dtype=jnp.int32)
    slot_step = jax.random.randint(jax.random.fold_in(base_key, 6), (), 0, QPG - 1, dtype=jnp.int32)
    second_slot = (first_slot + 1 + slot_step) % QPG
    targets = targets.at[group_pick, first_slot].set(0)
    targets = targets.at[group_pick, second_slot].set(CAPTIONS - 1)
    position = jnp.argsort(caption_order).astype(jnp.int32)
    caption_cluster = jnp.minimum(position // per_cluster, cluster_count - 1)
    image_cluster = caption_cluster[targets]
    centres = jax.random.truncated_normal(jax.random.fold_in(base_key, 8), -4.0, 4.0, (cluster_count, EMB), jnp.float32)
    return (targets, image_cluster, caption_cluster, centres)


def draw_targets(key, part):
    return cluster_plan(key)[0]


def draw_images(key, part):
    targets, image_cluster, caption_cluster, centres = cluster_plan(key)
    own_key = jax.random.fold_in(key, 7101)
    channel_ids = jnp.arange(C, dtype=jnp.int32) % EMB
    pattern = centres[image_cluster][:, :, channel_ids]
    strength = jnp.exp(jax.random.uniform(jax.random.fold_in(own_key, 1), (GROUPS, QPG, 1), jnp.float32, math.log(0.5), math.log(4.0)))
    own_part = jax.random.truncated_normal(jax.random.fold_in(own_key, 2), -4.0, 4.0, (GROUPS, QPG, C), jnp.float32)
    jitter = jax.random.truncated_normal(jax.random.fold_in(own_key, 3), -4.0, 4.0, (GROUPS, QPG, SIDE, SIDE, C), jnp.float32)
    mean_part = strength * pattern + own_part
    return (mean_part[:, :, None, None, :] + jitter).astype(jnp.bfloat16)


def draw_captions(key, part):
    targets, image_cluster, caption_cluster, centres = cluster_plan(key)
    own_key = jax.random.fold_in(key, 7201)
    strength = jnp.exp(jax.random.uniform(jax.random.fold_in(own_key, 1), (CAPTIONS, 1), jnp.float32, math.log(0.5), math.log(2.0)))
    jitter = jax.random.truncated_normal(jax.random.fold_in(own_key, 2), -4.0, 4.0, (CAPTIONS, EMB), jnp.float32)
    return (strength * centres[caption_cluster] + jitter).astype(jnp.bfloat16)


def draw_projection(key, part):
    own_key = jax.random.fold_in(key, 7301)
    spread = jax.random.truncated_normal(own_key, -4.0, 4.0, (C, EMB), jnp.float32)
    diagonal = (lax.broadcasted_iota(jnp.int32, (C, EMB), 0) == lax.broadcasted_iota(jnp.int32, (C, EMB), 1)).astype(jnp.float32)
    return (spread * (1.0 / math.sqrt(C)) + 2.0 * diagonal).astype(jnp.bfloat16)


def scatter_about(rng, extent, width, most, kind=jnp.bfloat16):
    entries = width * jax.random.normal(rng, extent, jnp.float32)
    return jnp.clip(entries, min=-most, max=most).astype(kind)


def setup_inputs(seed: int = 0) -> dict:
    streams_of = jax.random.split(jax.random.key(seed), 6)
    return {
        "images": draw_images(jax.random.fold_in(streams_of[5], 71), 0),
        "targets": draw_targets(jax.random.fold_in(streams_of[5], 71), 0),
        "kernel": scatter_about(streams_of[2], (KS, KS, C), KK ** -0.5, 0.875),
        "projection": draw_projection(jax.random.fold_in(streams_of[5], 71), 0),
        "captions": draw_captions(jax.random.fold_in(streams_of[5], 71), 0),
    }


logit_sharpness = 20.0

def depthwise(padded, kernel):
    reach = kernel.shape[0]
    side = padded.shape[1] - reach + 1
    total = jnp.zeros((padded.shape[0], side, side, padded.shape[3]), jnp.float32)
    for row_off in range(reach):
        for col_off in range(reach):
            window = padded[:, row_off:row_off + side, col_off:col_off + side, :].astype(jnp.float32)
            total = total + window * kernel[row_off, col_off].astype(jnp.float32)
    return total

def forward(pixels, kernel, projection):
    margin = kernel.shape[0] // 2
    padded = jnp.pad(pixels, ((0, 0), (margin, margin), (margin, margin), (0, 0)))
    hidden = depthwise(padded, kernel)
    centre = hidden - lax.optimization_barrier(jnp.mean(hidden, -1, keepdims=True))
    scale_inv = lax.rsqrt(lax.optimization_barrier(jnp.mean(centre * centre, -1, keepdims=True)) + 1e-06)
    normed = centre * scale_inv
    pooled = lax.optimization_barrier(jnp.mean(pixels.astype(jnp.float32) + normed, axis=(1, 2))).astype(jnp.bfloat16)
    embedded = jnp.dot(pooled, projection, preferred_element_type=jnp.float32)
    inv_norm = lax.rsqrt(lax.optimization_barrier(jnp.sum(embedded * embedded, -1, keepdims=True)) + 1e-06)
    return (padded, normed, scale_inv, embedded, inv_norm)

def backward(padded, normed, scale_inv, embedded, inv_norm, kernel, projection, query_gradient):
    unit = embedded * inv_norm
    emb_grad = ((query_gradient - unit * lax.optimization_barrier(jnp.sum(unit * query_gradient, -1, keepdims=True))) * inv_norm).astype(jnp.bfloat16)
    pooled_grad = lax.dot_general(emb_grad, projection, (((1,), (1,)), ((), ())), preferred_element_type=jnp.float32)
    side = normed.shape[1]
    out_grad = (pooled_grad / (side * side))[:, None, None, :]
    hidden_grad = scale_inv * (out_grad - lax.optimization_barrier(jnp.mean(out_grad, -1, keepdims=True)) - normed * lax.optimization_barrier(jnp.mean(normed * out_grad, -1, keepdims=True)))
    reach = kernel.shape[0]
    margin = reach // 2
    grad_pad = jnp.pad(hidden_grad, ((0, 0), (margin, margin), (margin, margin), (0, 0)))
    input_grad = out_grad + depthwise(grad_pad, kernel[::-1, ::-1])
    taps = []
    for row_off in range(reach):
        for col_off in range(reach):
            window = padded[:, row_off:row_off + side, col_off:col_off + side, :].astype(jnp.float32)
            taps.append(lax.optimization_barrier(jnp.sum(window * hidden_grad, axis=(0, 1, 2))))
    return (input_grad, jnp.stack(taps, 0).T)

def normalize(captions):
    values = captions.astype(jnp.float32)
    return (values * lax.rsqrt(lax.optimization_barrier(jnp.sum(values * values, -1, keepdims=True)) + 1e-06)).astype(jnp.bfloat16)

def reference(images, targets, kernel, projection, captions):
    blocks = images.reshape((-1, IMG_DEV) + images.shape[2:])

    def embed_block(pixels):
        padded, normed, scale_inv, embedded, inv_norm = forward(pixels, kernel, projection)
        return (embedded * inv_norm).astype(jnp.bfloat16)
    query_vectors = lax.map(embed_block, blocks).reshape(-1, EMB)
    normalized_caption_vectors = normalize(captions)
    similarity_scores = logit_sharpness * lax.dot_general(query_vectors, normalized_caption_vectors, (((1,), (1,)), ((), ())), preferred_element_type=jnp.float32)
    col_log = jnp.log(lax.optimization_barrier(jnp.sum(jnp.exp(similarity_scores), 0)))
    weight = jnp.exp(similarity_scores - col_log)
    row_sum = lax.optimization_barrier(jnp.sum(weight, 1))
    flat_targets = targets.reshape(-1).astype(jnp.int32)
    target_logit = jnp.take_along_axis(similarity_scores, flat_targets[:, None], 1)[:, 0] - col_log[flat_targets]
    loss = jnp.log(row_sum) - target_logit
    count = flat_targets.shape[0]
    grad = weight / row_sum[:, None]
    grad = grad.at[jnp.arange(count, dtype=jnp.int32), flat_targets].add(-1.0)
    col_grad = lax.optimization_barrier(jnp.sum(grad, 0))
    similarity_gradient = (grad - weight * col_grad).astype(jnp.bfloat16)
    query_gradient = logit_sharpness * jnp.dot(similarity_gradient, normalized_caption_vectors, preferred_element_type=jnp.float32)
    grad_blocks = query_gradient.reshape(-1, IMG_DEV, EMB)

    def back_block(pair):
        pixels, block_grad = pair
        padded, normed, scale_inv, embedded, inv_norm = forward(pixels, kernel, projection)
        input_grad, kernel_terms = backward(padded, normed, scale_inv, embedded, inv_norm, kernel, projection, block_grad)
        return (input_grad.astype(jnp.bfloat16), kernel_terms)
    input_grads, kernel_terms = lax.map(back_block, (blocks, grad_blocks))
    kernel_grad = lax.optimization_barrier(jnp.sum(kernel_terms, 0))
    return (loss.reshape(targets.shape), input_grads.reshape(images.shape), kernel_grad)
```

```python
import jax
import jax.numpy as jnp
from jax import lax
from jax.experimental import pallas as pl
from jax.experimental.pallas import tpu as pltpu
from jax.sharding import PartitionSpec as P

MESH = pl.DeviceIdType.MESH
f32, bf16 = jnp.float32, jnp.bfloat16

SCALE = 20.0
EPS = 1e-06
C, D, S = 1536, 768, 7
T = C // 128
PIX = S * S
L, G = 32, 8
N = 8
H = L // 2
Q = L * N
CAPS = 4096
CH = 512
NCH = CAPS // CH


def remote(src, dst, send, recv, where):
    return pltpu.make_async_remote_copy(
        src_ref=src, dst_ref=dst, send_sem=send, recv_sem=recv, device_id=where, device_id_type=MESH
    )


def hop(pos, k):
    step, low = k // 2, k % 2
    half = (step + 1) // 2
    z = (pos // 2 + 4 + half * (2 * (step % 2) - 1)) % 8
    return z * 2 + (pos + low) % 2


def conv_rows(load, tap, flip):
    for i in range(S):
        acc = [None] * S
        for a in range(S):
            r = i + a - 3
            if not 0 <= r < S:
                continue
            row = [load(r, x) for x in range(S)]
            for b in range(S):
                w = tap(S - 1 - a, S - 1 - b) if flip else tap(a, b)
                for j in range(S):
                    x = j + b - 3
                    if 0 <= x < S:
                        term = row[x] * w
                        acc[j] = term if acc[j] is None else acc[j] + term
        yield i, acc


def mega(
    img_hbm, tgt_ref, ker_ref, proj_hbm, cap_hbm,
    loss_ref, ig_ref, kg_ref,
    img, proj, u, xf, kf, tmp, nf, rsb, xs,
    qslots, qb, tcol, iot, cnt, e, irc, sgb, cols, cols2, rows,
    pacc, prec, rsend, rrec, dkr, kgt, kps, kprec, krec, krec2,
    in_sem, ag_s, ag_r, fw_s, c1_s, c1_r, c2_s, c2_r, rw_s, rw_r,
    pp_s, pp_r, rs_s, rs_r, kp_s, kp_r, ks_s, ks_r, k2_s, k2_r,
):
    me = lax.axis_index("loop")
    grp = lax.axis_index("group")
    core, pos = me % 2, me // 2
    mate = {"loop": me + 1 - 2 * core}
    slot = core * H + pos

    def peer(p):
        return {"loop": p * 2 + core}

    c_img = pltpu.make_async_copy(img_hbm, img, in_sem.at[0])
    c_proj = pltpu.make_async_copy(proj_hbm, proj, in_sem.at[1])
    c_cap = pltpu.make_async_copy(cap_hbm, u, in_sem.at[2])
    c_img.start()
    c_proj.start()
    c_cap.start()
    barrier = pltpu.get_barrier_semaphore()

    def greet_loop(k, carry):
        pl.semaphore_signal(barrier, inc=1, device_id={"loop": (me + k) % L}, device_id_type=MESH)
        return carry

    def greet_group(k, carry):
        pl.semaphore_signal(barrier, inc=1, device_id={"group": (grp + k) % G}, device_id_type=MESH)
        return carry

    lax.fori_loop(1, L, greet_loop, 0)
    lax.fori_loop(1, G, greet_group, 0)

    def lanes(t):
        return pl.ds(pl.multiple_of(t * 128, 128), 128)

    c_img.wait()

    def forward_tile(t, carry):
        for n in range(N):
            for i in range(S):
                tmp[n * 56 + i * 8 : n * 56 + i * 8 + S, :] = img[n, i, :, lanes(t)].astype(f32)
        for a in range(S):
            kf[t, a * 8 : a * 8 + S, :] = ker_ref[a, :, lanes(t)].astype(f32)
        total = None
        for i in range(S):
            for j in range(S):
                v = tmp[pl.ds(i * 8 + j, N, stride=56), :]
                xf[t, i * S + j] = v
                total = v if total is None else total + v
        xs[t] = total
        for i, acc in conv_rows(
            lambda r, x: xf[t, r * S + x],
            lambda a, b: jnp.broadcast_to(kf[t, a * 8 + b : a * 8 + b + 1, :], (N, 128)),
            False,
        ):
            for j in range(S):
                nf[t, i * S + j] = acc[j]
        return carry

    lax.fori_loop(0, T, forward_tile, 0)

    def norm_row(i, acc):
        for j in range(S):
            p = i * S + j
            h = nf[:, p]
            mu = jnp.sum(jnp.sum(h, axis=0), axis=1, keepdims=True) * (1.0 / C)
            cen = h - mu[None]
            var = jnp.sum(jnp.sum(cen * cen, axis=0), axis=1, keepdims=True) * (1.0 / C)
            rs = lax.rsqrt(var + EPS)
            rsb[p] = jnp.broadcast_to(rs, (N, 128))
            nrm = cen * rs[None]
            nf[:, p] = nrm
            acc = acc + nrm
        return acc

    nsum = lax.fori_loop(0, S, norm_row, xs[...])
    pooled = (nsum * (1.0 / PIX)).astype(bf16)
    pooled = jnp.concatenate([pooled[t] for t in range(T)], axis=1)
    c_proj.wait()
    embedded = jnp.dot(pooled, proj[...], preferred_element_type=f32)
    inv_norm = lax.rsqrt(jnp.sum(embedded * embedded, axis=1, keepdims=True) + EPS)
    unit = embedded * inv_norm
    qslots[slot] = unit.astype(bf16)

    pl.semaphore_wait(barrier, L - 1 + G - 1)
    own_q = qslots.at[slot]

    def ag_send(k, carry):
        to = hop(pos, k + k // (H - 2))
        remote(own_q, own_q, ag_s.at[k], ag_r.at[slot], peer(to)).start()
        return carry

    lax.fori_loop(0, H - 1, ag_send, 0)
    remote(own_q, own_q, fw_s.at[0], ag_r.at[slot], mate).start()

    c_cap.wait()

    def unit_rows(r, carry):
        rng = pl.ds(pl.multiple_of(r * 128, 128), 128)
        v = u[rng, :].astype(f32)
        u[rng, :] = (v * lax.rsqrt(jnp.sum(v * v, axis=1, keepdims=True) + EPS)).astype(bf16)
        return carry

    lax.fori_loop(0, CAPS // 128, unit_rows, 0)
    local = (tgt_ref[...] - me * CAPS).astype(f32)
    for h in range(2):
        col = jnp.transpose(jnp.broadcast_to(local[:, h * 128 : h * 128 + 128], (128, 128)))
        for b in range(16):
            l = h * 16 + b
            s = (l % 2) * H + l // 2
            tcol[s * N : s * N + N, :] = col[b * N : b * N + N, :]
    iot[...] = lax.broadcasted_iota(jnp.int32, (N, CH), 1).astype(f32)

    def wide(x):
        return jnp.concatenate([x] * (CH // 128), axis=1)

    def hits(r, rng):
        ids = iot[0:1, :] + (r * CH).astype(f32)
        return wide(tcol[rng, :]) == ids

    def count(r, carry):
        cnt[pl.ds(r, 1), :] = jnp.sum(jnp.where(hits(r, slice(None)), 1.0, 0.0), axis=0, keepdims=True)
        return carry

    lax.fori_loop(0, NCH, count, 0)

    def ag_forward(k, carry):
        frm = core * H + (pos + k) % H
        got = qslots.at[frm]
        remote(got, got, ag_s.at[0], ag_r.at[frm], mate).wait_recv()
        remote(got, got, fw_s.at[k], ag_r.at[frm], mate).start()
        return carry

    lax.fori_loop(1, H, ag_forward, 0)

    def ag_mate(k, carry):
        frm = (1 - core) * H + k
        got = qslots.at[frm]
        remote(got, got, ag_s.at[0], ag_r.at[frm], mate).wait_recv()
        return carry

    lax.fori_loop(0, H, ag_mate, 0)

    def ag_done(k, carry):
        remote(own_q, own_q, ag_s.at[k], ag_r.at[0], mate).wait_send()
        return carry

    def fw_done(k, carry):
        remote(own_q, own_q, fw_s.at[k], ag_r.at[0], mate).wait_send()
        return carry

    qb[...] = qslots[...].astype(f32).reshape(Q, D).astype(bf16)

    def scores(r, carry):
        rng = pl.ds(pl.multiple_of(r * CH, CH), CH)
        s = lax.dot_general(qb[...], u[rng, :], (((1,), (1,)), ((), ())), preferred_element_type=f32)
        v = jnp.exp(SCALE * s)
        e[r] = v
        cols[grp, pl.ds(r, 1), :] = jnp.sum(v, axis=0, keepdims=True)
        return carry

    lax.fori_loop(0, NCH, scores, 0)
    lax.fori_loop(0, H - 1, ag_done, 0)
    lax.fori_loop(0, H, fw_done, 0)

    def group_exchange(buf, send, recv):
        own = buf.at[grp]

        def start(k, carry):
            remote(own, own, send.at[k], recv.at[grp], {"group": (grp + k) % G}).start()
            return carry

        def arrive(k, carry):
            frm = (grp + k) % G
            remote(own, buf.at[frm], send.at[k], recv.at[frm], {"group": frm}).wait()
            return carry

        lax.fori_loop(1, G, start, 0)
        return lambda: lax.fori_loop(1, G, arrive, 0)

    group_exchange(cols, c1_s, c1_r)()
    ic = 1.0 / jnp.sum(cols[...], axis=0)
    cols[0] = ic

    def row_pass(r, carry):
        acc, hit = carry
        w = e[r] * cols[0, pl.ds(r, 1), :]
        z = jnp.where(hits(r, slice(None)), w, 0.0)
        for b in range(CH // 128):
            acc = acc + w[:, b * 128 : b * 128 + 128]
            hit = hit + z[:, b * 128 : b * 128 + 128]
        return acc, hit

    zero = jnp.zeros((Q, 128), f32)
    acc, hit = lax.fori_loop(0, NCH, row_pass, (zero, zero))
    parts = [
        jnp.sum(jnp.transpose(x[h * 128 : h * 128 + 128, :]), axis=0, keepdims=True)
        for x in (acc, hit)
        for h in range(2)
    ]
    rows[me] = jnp.concatenate(parts + [jnp.zeros((4, 128), f32)], axis=0)
    own_r = rows.at[me]

    def row_start(k, carry):
        j = k + k // (L - 4)
        to = hop(pos, j // 2) * 2 + (core + j) % 2
        remote(own_r, own_r, rw_s.at[k], rw_r.at[me], {"loop": to}).start()
        return carry

    def row_wait(k, carry):
        frm = (me + k) % L
        remote(own_r, rows.at[frm], rw_s.at[k - 1], rw_r.at[frm], {"loop": frm}).wait()
        return carry

    lax.fori_loop(0, L - 1, row_start, 0)
    lax.fori_loop(1, L, row_wait, 0)
    tot = jnp.sum(rows[...], axis=0)

    def spread(x):
        return jnp.transpose(jnp.broadcast_to(x, (128, 128)))

    inv = 1.0 / tot[0:2]
    for h in range(2):
        irc[h * 128 : h * 128 + 128, :] = spread(inv[h : h + 1])

    def grad_pass(r, carry):
        y = e[r] * wide(irc[...])
        cols2[grp, pl.ds(r, 1), :] = (
            jnp.sum(y, axis=0, keepdims=True) * cols[0, pl.ds(r, 1), :] - cnt[pl.ds(r, 1), :]
        )
        return carry

    lax.fori_loop(0, NCH, grad_pass, 0)
    finish = group_exchange(cols2, c2_s, c2_r)
    los = jnp.log(tot[0:2]) - jnp.log(tot[2:4])
    for h in range(2):
        zer = spread(los[h : h + 1])
        tmp[h * 128 : h * 128 + 128, :] = zer
    loss_ref[...] = tmp[pl.ds(pl.multiple_of(slot * N, N), N), :]
    finish()
    cols2[0] = jnp.sum(cols2[...], axis=0)

    def half_grad(c):
        rng = pl.ds(pl.multiple_of(c * 128, 128), 128)

        def chunk(r, carry):
            base = wide(irc[rng, :]) - cols2[0, pl.ds(r, 1), :]
            g = e[r, rng, :] * (cols[0, pl.ds(r, 1), :] * base)
            g = g - jnp.where(hits(r, rng), 1.0, 0.0)
            sgb[:, pl.ds(pl.multiple_of(r * CH, CH), CH)] = g.astype(bf16)
            return carry

        lax.fori_loop(0, NCH, chunk, 0)
        return SCALE * jnp.dot(sgb[...], u[...], preferred_element_type=f32)

    pacc[...] = half_grad(1 - core).reshape(H, N, D)
    to_mate = remote(pacc, prec, pp_s, pp_r, mate)
    to_mate.start()
    mine = half_grad(core).reshape(H, N, D)
    to_mate.wait()
    rsend[...] = mine + prec[...]

    def scatter_start(src, dst, send, recv):
        def start(k, carry):
            to = hop(pos, k + k // (H - 2))
            remote(src.at[to], dst.at[pos], send.at[k], recv.at[pos], peer(to)).start()
            return carry

        lax.fori_loop(0, H - 1, start, 0)

    def scatter_wait(src, dst, send, recv):
        def arrive(k, carry):
            frm = (pos + k) % H
            remote(src.at[frm], dst.at[frm], send.at[k - 1], recv.at[frm], peer(frm)).wait()
            return carry

        lax.fori_loop(1, H, arrive, 0)

    rrec[pos] = rsend[pos]
    scatter_start(rsend, rrec, rs_s, rs_r)
    scatter_wait(rsend, rrec, rs_s, rs_r)
    qg = jnp.sum(rrec[...], axis=0)

    eg = ((qg - unit * jnp.sum(unit * qg, axis=1, keepdims=True)) * inv_norm).astype(bf16)
    pg = lax.dot_general(eg, proj[...], (((1,), (1,)), ((), ())), preferred_element_type=f32)
    og = pg * (1.0 / PIX)
    centred = og - jnp.sum(og, axis=1, keepdims=True) * (1.0 / C)
    for t in range(T):
        xs[t] = og[:, t * 128 : t * 128 + 128]
        dkr[t, 0:N, :] = centred[:, t * 128 : t * 128 + 128]

    def hidden_row(i, carry):
        for j in range(S):
            p = i * S + j
            nrm = nf[:, p]
            m2 = jnp.sum(jnp.sum(nrm * xs[...], axis=0), axis=1, keepdims=True) * (1.0 / C)
            nf[:, p] = rsb[p][None] * (dkr[:, 0:N, :] - nrm * m2[None])
        return carry

    lax.fori_loop(0, S, hidden_row, 0)

    def kernel_tile(t, carry):
        dkr[t, 48:64, :] = jnp.zeros((16, 128), f32)
        for a in range(S):
            acc = [None] * S
            for i in range(S):
                r = i + a - 3
                if not 0 <= r < S:
                    continue
                x = [xf[t, r * S + c] for c in range(S)]
                g = [nf[t, i * S + c] for c in range(S)]
                for b in range(S):
                    for j in range(S):
                        c = j + b - 3
                        if 0 <= c < S:
                            term = x[c] * g[j]
                            acc[b] = term if acc[b] is None else acc[b] + term
            for b in range(S):
                dkr[t, a * S + b : a * S + b + 1, :] = jnp.sum(acc[b], axis=0, keepdims=True)
        flat = jnp.concatenate([dkr[t], jnp.zeros((64, 128), f32)], axis=0)
        kgt[lanes(t), :] = jnp.transpose(flat)
        return carry

    lax.fori_loop(0, T, kernel_tile, 0)

    def pack(l, carry):
        c = l % 2
        low = kgt[pl.ds(pl.multiple_of(l * 48, 8), 24), :]
        high = kgt[pl.ds(pl.multiple_of(l * 48 + 24, 8), 24), :]
        kps[c * H + l // 2] = low + pltpu.roll(high, 64, 1)
        return carry

    lax.fori_loop(0, L, pack, 0)
    other = pl.ds((1 - core) * H, H)
    k_mate = remote(kps.at[other], kprec, kp_s, kp_r, mate)
    k_mate.start()

    def image_tile(t, carry):
        for i, acc in conv_rows(
            lambda r, x: nf[t, r * S + x],
            lambda a, b: jnp.broadcast_to(kf[t, a * 8 + b : a * 8 + b + 1, :], (N, 128)),
            True,
        ):
            for j in range(S):
                tmp[pl.ds(i * 8 + j, N, stride=56), :] = acc[j] + xs[t]
        for n in range(N):
            for i in range(S):
                ig_ref[n, i, :, lanes(t)] = tmp[n * 56 + i * 8 : n * 56 + i * 8 + S, :].astype(bf16)
        return carry

    lax.fori_loop(0, 3, image_tile, 0)
    k_mate.wait()
    ksum = kps.at[pl.ds(core * H, H)]
    kprec[...] = kprec[...] + ksum[...]
    krec[pos] = kprec[pos]
    scatter_start(kprec, krec, ks_s, ks_r)
    lax.fori_loop(3, T, image_tile, 0)
    scatter_wait(kprec, krec, ks_s, ks_r)
    krec2[grp] = jnp.sum(krec[...], axis=0)
    group_exchange(krec2, k2_s, k2_r)()
    kg_ref[...] = jnp.sum(krec2[...], axis=0)


def shards(images, targets, kernel, projection, captions):
    vmem = pltpu.VMEM
    dma = pltpu.SemaphoreType.DMA
    anyspace = pl.BlockSpec(memory_space=pl.ANY)
    whole = pl.BlockSpec(memory_space=vmem)
    scratch = [
        vmem((N, S, S, C), bf16),
        vmem((C, D), bf16),
        vmem((CAPS, D), bf16),
        vmem((T, PIX, N, 128), f32),
        vmem((T, 56, 128), f32),
        vmem((N * 56, 128), f32),
        vmem((T, PIX, N, 128), f32),
        vmem((PIX, N, 128), f32),
        vmem((T, N, 128), f32),
        vmem((L, N, D), bf16),
        vmem((Q, D), bf16),
        vmem((Q, 128), f32),
        vmem((N, CH), f32),
        vmem((NCH, CH), f32),
        vmem((NCH, Q, CH), f32),
        vmem((Q, 128), f32),
        vmem((Q // 2, CAPS), bf16),
        vmem((G, NCH, CH), f32),
        vmem((G, NCH, CH), f32),
        vmem((L, 8, 128), f32),
        vmem((H, N, D), f32),
        vmem((H, N, D), f32),
        vmem((H, N, D), f32),
        vmem((H, N, D), f32),
        vmem((T, 64, 128), f32),
        vmem((C, 128), f32),
        vmem((L, 24, 128), f32),
        vmem((H, 24, 128), f32),
        vmem((H, 24, 128), f32),
        vmem((G, 24, 128), f32),
        dma((3,)), dma((H,)), dma((L,)), dma((H,)),
        dma((G,)), dma((G,)), dma((G,)), dma((G,)),
        dma((L,)), dma((L,)),
        dma, dma, dma((H,)), dma((H,)),
        dma, dma, dma((H,)), dma((H,)), dma((G,)), dma((G,)),
    ]
    loss, image_grad, kg = pl.pallas_call(
        mega,
        name="mega",
        out_shape=(
            jax.ShapeDtypeStruct((N, 128), f32),
            jax.ShapeDtypeStruct((N, S, S, C), bf16),
            jax.ShapeDtypeStruct((24, 128), f32),
        ),
        in_specs=[anyspace, whole, whole, anyspace, anyspace],
        out_specs=(whole, whole, whole),
        scratch_shapes=scratch,
        compiler_params=pltpu.CompilerParams(
            collective_id=0, has_side_effects=True, vmem_limit_bytes=60 * 1024 * 1024
        ),
    )(images[0], targets, kernel, projection, captions)
    own = jnp.concatenate([kg[:, 0:PIX], kg[:, 64 : 64 + PIX]], axis=0)
    kernel_share = lax.dynamic_slice_in_dim(own, lax.axis_index("group") * 6, 6, 0)
    return loss[:, 0][None], image_grad[None], kernel_share


def solution(mesh):
    placed = (P("group", "loop", None, None, None), P("group", None), P(), P(), P("loop", None))
    return jax.shard_map(
        shards,
        mesh=mesh,
        in_specs=placed,
        out_specs=(
            P("group", "loop"),
            P("group", "loop", None, None, None),
            P(("loop", "group"), None),
        ),
        check_vma=False,
    )
```

```python
import jax
import jax.numpy as jnp
from jax import lax
from jax.experimental import pallas as pl
from jax.experimental.pallas import tpu as pltpu
from jax.sharding import PartitionSpec as P

MESH = pl.DeviceIdType.MESH
ORDER = (4, 5, 3, 6, 2, 7, 1, 0)
f32, bf16 = jnp.float32, jnp.bfloat16

SCALE = 20.0
EPS = 1e-06
C, D, S = 1536, 768, 7
T = C // 128
PIX = S * S
L, G = 32, 8
N = 8
H = L // 2
Q = L * N
CAPS = 4096
CH = 512
NCH = CAPS // CH


def remote(src, dst, send, recv, where):
    return pltpu.make_async_remote_copy(
        src_ref=src, dst_ref=dst, send_sem=send, recv_sem=recv, device_id=where, device_id_type=MESH
    )


def conv_rows(load, tap, flip):
    for i in range(S):
        acc = [None] * S
        for a in range(S):
            r = i + a - 3
            if not 0 <= r < S:
                continue
            row = [load(r, x) for x in range(S)]
            for b in range(S):
                w = tap(S - 1 - a, S - 1 - b) if flip else tap(a, b)
                for j in range(S):
                    x = j + b - 3
                    if 0 <= x < S:
                        term = row[x] * w
                        acc[j] = term if acc[j] is None else acc[j] + term
        yield i, acc


def mega(
    img_hbm, tgt_ref, ker_ref, proj_hbm, cap_hbm,
    loss_ref, ig_ref, kg_ref,
    img, proj, u, xf, kf, mub, nf, rsb, xs,
    qslots, qb, tcol, iot, cnt, e, irc, hit, pick, sgb, cols, cols2, rows,
    pacc, prec, rsend, rrec, dkr, kgt, kps, kprec, ksend, krec, krec2,
    in_sem, ag_s, ag_r, fw_s, c1_s, c1_r, c2_s, c2_r, rw_s, rw_r,
    pp_s, pp_r, rs_s, rs_r, kp_s, kp_r, ks_s, ks_r, k2_s, k2_r,
):
    me = lax.axis_index("loop")
    grp = lax.axis_index("group")
    core, pos = me % 2, me // 2
    mate = {"loop": me + 1 - 2 * core}
    slot = core * H + pos

    def peer(p):
        return {"loop": p * 2 + core}

    c_img = pltpu.make_async_copy(img_hbm, img, in_sem.at[0])
    c_proj = pltpu.make_async_copy(proj_hbm, proj, in_sem.at[1])
    c_cap = pltpu.make_async_copy(cap_hbm, u, in_sem.at[2])
    c_img.start()
    c_proj.start()
    c_cap.start()
    barrier = pltpu.get_barrier_semaphore()

    def greet_loop(k, carry):
        pl.semaphore_signal(barrier, inc=1, device_id={"loop": lax.rem(me + k, L)}, device_id_type=MESH)
        return carry

    def greet_group(k, carry):
        pl.semaphore_signal(barrier, inc=1, device_id={"group": lax.rem(grp + k, G)}, device_id_type=MESH)
        return carry

    lax.fori_loop(1, L, greet_loop, 0)
    lax.fori_loop(1, G, greet_group, 0)

    def lanes(t):
        return pl.ds(pl.multiple_of(t * 128, 128), 128)

    c_img.wait()

    def forward_tile(t, carry):
        for a in range(S):
            kf[t, a * 8 : a * 8 + S, :] = ker_ref[a, :, lanes(t)].astype(f32)
        total = None
        for p in range(PIX):
            v = img[p, :, lanes(t)].astype(f32)
            xf[t, p] = v
            total = v if total is None else total + v
        xs[t] = total
        for i, acc in conv_rows(
            lambda r, x: xf[t, r * S + x],
            lambda a, b: jnp.broadcast_to(kf[t, a * 8 + b : a * 8 + b + 1, :], (N, 128)),
            False,
        ):
            for j in range(S):
                nf[t, i * S + j] = acc[j]
        return carry

    lax.fori_loop(0, T, forward_tile, 0)

    def lane_mean(x):
        return jnp.broadcast_to(jnp.sum(x, axis=1, keepdims=True) * (1.0 / C), (N, 128))

    def mean_row(i, carry):
        for j in range(S):
            mub[i * S + j] = lane_mean(jnp.sum(nf[:, i * S + j], axis=0))
        return carry

    def var_row(i, carry):
        for j in range(S):
            p = i * S + j
            cen = nf[:, p] - mub[p][None]
            rsb[p] = lax.rsqrt(lane_mean(jnp.sum(cen * cen, axis=0)) + EPS)
        return carry

    def norm_row(i, acc):
        for j in range(S):
            p = i * S + j
            nrm = (nf[:, p] - mub[p][None]) * rsb[p][None]
            nf[:, p] = nrm
            acc = acc + nrm
        return acc

    lax.fori_loop(0, S, mean_row, 0)
    lax.fori_loop(0, S, var_row, 0)
    nsum = lax.fori_loop(0, S, norm_row, xs[...])
    pooled = (nsum * (1.0 / PIX)).astype(bf16)
    pooled = jnp.concatenate([pooled[t] for t in range(T)], axis=1)
    c_proj.wait()
    embedded = jnp.dot(pooled, proj[...], preferred_element_type=f32)
    inv_norm = lax.rsqrt(jnp.sum(embedded * embedded, axis=1, keepdims=True) + EPS)
    unit = embedded * inv_norm
    qslots[slot] = unit.astype(bf16)

    pl.semaphore_wait(barrier, L - 1 + G - 1)
    own_q = qslots.at[slot]

    def around(start):
        for k in range(H - 1):
            j = k + k // (H - 2)
            start(k, lax.rem(pos // 2 + ORDER[j // 2], 8) * 2 + lax.rem(pos % 2 + j % 2, 2))

    around(lambda k, to: remote(own_q, own_q, ag_s.at[k], ag_r.at[slot], peer(to)).start())
    remote(own_q, own_q, fw_s.at[0], ag_r.at[slot], mate).start()

    c_cap.wait()

    def unit_rows(r, carry):
        rng = pl.ds(pl.multiple_of(r * 128, 128), 128)
        v = u[rng, :].astype(f32)
        u[rng, :] = (v * lax.rsqrt(jnp.sum(v * v, axis=1, keepdims=True) + EPS)).astype(bf16)
        return carry

    lax.fori_loop(0, CAPS // 128, unit_rows, 0)
    local = (tgt_ref[...] - me * CAPS).astype(f32)
    for h in range(2):
        col = jnp.transpose(jnp.broadcast_to(local[:, h * 128 : h * 128 + 128], (128, 128)))
        for b in range(16):
            l = h * 16 + b
            s = (l % 2) * H + l // 2
            tcol[s * N : s * N + N, :] = col[b * N : b * N + N, :]
    iot[...] = lax.broadcasted_iota(jnp.int32, (N, CH), 1).astype(f32)

    def wide(x):
        return jnp.concatenate([x] * (CH // 128), axis=1)

    def hits(r, rng):
        ids = iot[0:1, :] + (r * float(CH) if isinstance(r, int) else (r * CH).astype(f32))
        return wide(tcol[rng, :]) == ids

    def count(r, carry):
        cnt[pl.ds(r, 1), :] = jnp.sum(jnp.where(hits(r, slice(None)), 1.0, 0.0), axis=0, keepdims=True)
        return carry


    def ag_forward(k, carry):
        frm = core * H + lax.rem(pos + k, H)
        got = qslots.at[frm]
        remote(got, got, ag_s.at[0], ag_r.at[frm], mate).wait_recv()
        remote(got, got, fw_s.at[k], ag_r.at[frm], mate).start()
        return carry

    lax.fori_loop(1, H, ag_forward, 0)

    def ag_mate(k, carry):
        frm = (1 - core) * H + k
        got = qslots.at[frm]
        remote(got, got, ag_s.at[0], ag_r.at[frm], mate).wait_recv()
        return carry

    lax.fori_loop(0, H, ag_mate, 0)

    def ag_done(k, carry):
        remote(own_q, own_q, ag_s.at[k], ag_r.at[0], mate).wait_send()
        return carry

    def fw_done(k, carry):
        remote(own_q, own_q, fw_s.at[k], ag_r.at[0], mate).wait_send()
        return carry

    qb[...] = qslots[...].astype(f32).reshape(Q, D).astype(bf16)

    def scores(r, carry):
        rng = pl.ds(pl.multiple_of(r * CH, CH), CH)
        s = lax.dot_general(qb[...], u[rng, :], (((1,), (1,)), ((), ())), preferred_element_type=f32)
        v = jnp.exp(SCALE * s)
        e[r] = v
        cols[grp, pl.ds(r, 1), :] = jnp.sum(v, axis=0, keepdims=True)
        return carry

    lax.fori_loop(0, NCH, scores, 0)
    lax.fori_loop(0, H - 1, ag_done, 0)
    lax.fori_loop(0, H, fw_done, 0)

    def group_exchange(buf, send, recv):
        own = buf.at[grp]

        def start(k, carry):
            remote(own, own, send.at[k], recv.at[grp], {"group": lax.rem(grp + k, G)}).start()
            return carry

        def arrive(k, carry):
            frm = lax.rem(grp + k, G)
            remote(own, buf.at[frm], send.at[k], recv.at[frm], {"group": frm}).wait()
            return carry

        lax.fori_loop(1, G, start, 0)
        return lambda: lax.fori_loop(1, G, arrive, 0)

    def picked(c, carry):
        rng = pl.ds(pl.multiple_of(c * 128, 128), 128)

        def chunk(r, carry):
            sgb[:, pl.ds(pl.multiple_of(r * CH, CH), CH)] = jnp.where(hits(r, rng), 1.0, 0.0).astype(bf16)
            return carry

        lax.fori_loop(0, NCH, chunk, 0)
        pick[c] = jnp.dot(sgb[...], u[...], preferred_element_type=f32)
        return carry

    finish = group_exchange(cols, c1_s, c1_r)
    lax.fori_loop(0, NCH, count, 0)
    lax.fori_loop(0, 2, picked, 0)
    finish()
    ic = 1.0 / jnp.sum(cols[...], axis=0)
    cols[0] = ic

    def row_pass(q, carry):
        rng = pl.ds(pl.multiple_of(q * 32, 32), 32)
        acc = None
        for r in range(NCH):
            w = e[r, rng, :] * cols[0, r : r + 1, :]
            for b in range(CH // 128):
                v = w[:, b * 128 : b * 128 + 128]
                acc = v if acc is None else acc + v
        irc[rng, :] = acc
        return carry

    lax.fori_loop(0, Q // 32, row_pass, 0)
    rows[me] = jnp.concatenate(
        [jnp.sum(jnp.transpose(irc[h * 128 : h * 128 + 128, :]), axis=0, keepdims=True) for h in range(2)], axis=0
    )
    own_r = rows.at[me]

    for k in range(L):
        zo, low = ORDER[k // 4], k % 4
        if zo == 0 and low == 0:
            continue
        to = (lax.rem(pos // 2 + zo, 8) * 2 + lax.rem(pos % 2 + low // 2, 2)) * 2 + lax.rem(core + low % 2, 2)
        remote(own_r, own_r, rw_s.at[k], rw_r.at[me], {"loop": to}).start()

    def hit_pass(q, carry):
        rng = pl.ds(pl.multiple_of(q * 32, 32), 32)
        acc = None
        for r in range(NCH):
            z = jnp.where(hits(r, rng), e[r, rng, :] * cols[0, r : r + 1, :], 0.0)
            for b in range(CH // 128):
                v = z[:, b * 128 : b * 128 + 128]
                acc = v if acc is None else acc + v
        hit[rng, :] = acc
        return carry

    lax.fori_loop(0, Q // 32, hit_pass, 0)

    def row_wait(k, carry):
        frm = lax.rem(me + k, L)
        remote(own_r, rows.at[frm], rw_s.at[0], rw_r.at[frm], {"loop": frm}).wait_recv()
        return carry

    def row_sent(k, carry):
        remote(own_r, own_r, rw_s.at[k], rw_r.at[0], mate).wait_send()
        return carry

    lax.fori_loop(1, L, row_wait, 0)
    tot = jnp.sum(rows[...], axis=0)

    def spread(x):
        return jnp.transpose(jnp.broadcast_to(x, (128, 128)))

    inv = 1.0 / tot
    for h in range(2):
        irc[h * 128 : h * 128 + 128, :] = spread(inv[h : h + 1])

    def grad_pass(r, carry):
        y = e[r] * wide(irc[...])
        cols2[grp, pl.ds(r, 1), :] = (
            jnp.sum(y, axis=0, keepdims=True) * cols[0, pl.ds(r, 1), :] - cnt[pl.ds(r, 1), :]
        )
        return carry

    lax.fori_loop(0, NCH, grad_pass, 0)
    finish = group_exchange(cols2, c2_s, c2_r)
    for k in range(L):
        if k != ORDER.index(0) * 4:
            row_sent(k, 0)
    finish()
    cols2[0] = jnp.sum(cols2[...], axis=0)

    def half_grad(c):
        rng = pl.ds(pl.multiple_of(c * 128, 128), 128)

        def chunk(r, carry):
            base = wide(irc[rng, :]) - cols2[0, pl.ds(r, 1), :]
            g = e[r, rng, :] * (cols[0, pl.ds(r, 1), :] * base)
            sgb[:, pl.ds(pl.multiple_of(r * CH, CH), CH)] = g.astype(bf16)
            return carry

        lax.fori_loop(0, NCH, chunk, 0)
        return SCALE * (jnp.dot(sgb[...], u[...], preferred_element_type=f32) - pick[c])

    def with_hits(c):
        part = hit[pl.ds(pl.multiple_of(c * 128, 128), 128), :]
        return jnp.concatenate([half_grad(c), part], axis=1).reshape(H, N, D + 128)

    pacc[...] = with_hits(1 - core)
    to_mate = remote(pacc, prec, pp_s, pp_r, mate)
    to_mate.start()
    mine = with_hits(core)
    to_mate.wait()
    both = (mine + prec[...]).reshape(H * N, D + 128)
    found = jnp.broadcast_to(jnp.sum(both[:, D:], axis=1, keepdims=True), (H * N, 128))
    first = found.astype(bf16).astype(f32)
    second = (found - first).astype(bf16).astype(f32)
    lane = lax.broadcasted_iota(jnp.int32, (H * N, 128), 1)
    found = jnp.where(lane == 0, first, jnp.where(lane == 1, second, jnp.where(lane == 2, found - first - second, 0.0)))
    both = jnp.concatenate([both[:, 0:D], found], axis=1).reshape(H, N, D + 128)
    rsend[...] = both.astype(bf16)

    def scatter_start(src, dst, send, recv):
        around(lambda k, to: remote(src.at[to], dst.at[pos], send.at[k], recv.at[pos], peer(to)).start())

    def scatter_wait(src, dst, send, recv):
        def arrive(k, carry):
            frm = lax.rem(pos + k, H)
            remote(src.at[frm], dst.at[frm], send.at[k - 1], recv.at[frm], peer(frm)).wait()
            return carry

        lax.fori_loop(1, H, arrive, 0)

    rrec[pos] = rsend[pos]
    scatter_start(rsend, rrec, rs_s, rs_r)
    scatter_wait(rsend, rrec, rs_s, rs_r)
    qh = jnp.sum(rrec[...].astype(f32), axis=0)
    qg = qh[:, 0:D]
    own_rows = irc[pl.ds(pl.multiple_of(slot * N, N), N), :]
    loss_ref[...] = -jnp.log(own_rows) - jnp.log(jnp.sum(qh[:, D:], axis=1, keepdims=True))

    eg = ((qg - unit * jnp.sum(unit * qg, axis=1, keepdims=True)) * inv_norm).astype(bf16)
    pg = lax.dot_general(eg, proj[...], (((1,), (1,)), ((), ())), preferred_element_type=f32)
    og = pg * (1.0 / PIX)
    centred = og - jnp.sum(og, axis=1, keepdims=True) * (1.0 / C)
    for t in range(T):
        xs[t] = og[:, t * 128 : t * 128 + 128]
        dkr[t, 0:N, :] = centred[:, t * 128 : t * 128 + 128]

    def hidden_row(i, carry):
        for j in range(S):
            p = i * S + j
            nrm = nf[:, p]
            m2 = jnp.sum(jnp.sum(nrm * xs[...], axis=0), axis=1, keepdims=True) * (1.0 / C)
            nf[:, p] = rsb[p][None] * (dkr[:, 0:N, :] - nrm * m2[None])
        return carry

    lax.fori_loop(0, S, hidden_row, 0)

    def kernel_tile(t, carry):
        dkr[t, 48:64, :] = jnp.zeros((16, 128), f32)
        for a in range(S):
            acc = [None] * S
            for i in range(S):
                r = i + a - 3
                if not 0 <= r < S:
                    continue
                x = [xf[t, r * S + c] for c in range(S)]
                g = [nf[t, i * S + c] for c in range(S)]
                for b in range(S):
                    for j in range(S):
                        c = j + b - 3
                        if 0 <= c < S:
                            term = x[c] * g[j]
                            acc[b] = term if acc[b] is None else acc[b] + term
            for b in range(S):
                dkr[t, a * S + b : a * S + b + 1, :] = jnp.sum(acc[b], axis=0, keepdims=True)
        flat = jnp.concatenate([dkr[t], jnp.zeros((64, 128), f32)], axis=0)
        kgt[lanes(t), :] = jnp.transpose(flat)
        return carry

    lax.fori_loop(0, T, kernel_tile, 0)

    def pack(l, carry):
        c = l % 2
        low = kgt[pl.ds(pl.multiple_of(l * 48, 8), 24), :]
        high = kgt[pl.ds(pl.multiple_of(l * 48 + 24, 8), 24), :]
        kps[c * H + l // 2] = low + pltpu.roll(high, 64, 1)
        return carry

    lax.fori_loop(0, L, pack, 0)
    other = pl.ds((1 - core) * H, H)
    k_mate = remote(kps.at[other], kprec, kp_s, kp_r, mate)
    k_mate.start()

    def image_tile(t, carry):
        for i, acc in conv_rows(
            lambda r, x: nf[t, r * S + x],
            lambda a, b: jnp.broadcast_to(kf[t, a * 8 + b : a * 8 + b + 1, :], (N, 128)),
            True,
        ):
            for j in range(S):
                ig_ref[i * S + j, :, lanes(t)] = (acc[j] + xs[t]).astype(bf16)
        return carry

    lax.fori_loop(0, 3, image_tile, 0)
    k_mate.wait()
    ksum = kps.at[pl.ds(core * H, H)]
    ksend[...] = (kprec[...] + ksum[...]).astype(bf16)
    krec[pos] = ksend[pos]
    scatter_start(ksend, krec, ks_s, ks_r)
    lax.fori_loop(3, 9, image_tile, 0)
    scatter_wait(ksend, krec, ks_s, ks_r)
    krec2[grp] = jnp.sum(krec[...].astype(f32), axis=0)
    finish = group_exchange(krec2, k2_s, k2_r)
    lax.fori_loop(9, T, image_tile, 0)
    finish()
    kg_ref[...] = jnp.sum(krec2[...], axis=0)


def shards(images, targets, kernel, projection, captions):
    vmem = pltpu.VMEM
    dma = pltpu.SemaphoreType.DMA
    anyspace = pl.BlockSpec(memory_space=pl.ANY)
    whole = pl.BlockSpec(memory_space=vmem)
    scratch = [
        vmem((PIX, N, C), bf16),
        vmem((C, D), bf16),
        vmem((CAPS, D), bf16),
        vmem((T, PIX, N, 128), f32),
        vmem((T, 56, 128), f32),
        vmem((PIX, N, 128), f32),
        vmem((T, PIX, N, 128), f32),
        vmem((PIX, N, 128), f32),
        vmem((T, N, 128), f32),
        vmem((L, N, D), bf16),
        vmem((Q, D), bf16),
        vmem((Q, 128), f32),
        vmem((N, CH), f32),
        vmem((NCH, CH), f32),
        vmem((NCH, Q, CH), f32),
        vmem((Q, 128), f32),
        vmem((Q, 128), f32),
        vmem((2, Q // 2, D), f32),
        vmem((Q // 2, CAPS), bf16),
        vmem((G, NCH, CH), f32),
        vmem((G, NCH, CH), f32),
        vmem((L, 2, 128), f32),
        vmem((H, N, D + 128), f32),
        vmem((H, N, D + 128), f32),
        vmem((H, N, D + 128), bf16),
        vmem((H, N, D + 128), bf16),
        vmem((T, 64, 128), f32),
        vmem((C, 128), f32),
        vmem((L, 24, 128), f32),
        vmem((H, 24, 128), f32),
        vmem((H, 24, 128), bf16),
        vmem((H, 24, 128), bf16),
        vmem((G, 24, 128), f32),
        dma((3,)), dma((H,)), dma((L,)), dma((H,)),
        dma((G,)), dma((G,)), dma((G,)), dma((G,)),
        dma((L,)), dma((L,)),
        dma, dma, dma((H,)), dma((H,)),
        dma, dma, dma((H,)), dma((H,)), dma((G,)), dma((G,)),
    ]
    loss, image_grad, kg = pl.pallas_call(
        mega,
        name="mega",
        out_shape=(
            jax.ShapeDtypeStruct((N, 128), f32),
            jax.ShapeDtypeStruct((PIX, N, C), bf16),
            jax.ShapeDtypeStruct((24, 128), f32),
        ),
        in_specs=[anyspace, whole, whole, anyspace, anyspace],
        out_specs=(whole, whole, whole),
        scratch_shapes=scratch,
        compiler_params=pltpu.CompilerParams(
            collective_id=0, has_side_effects=True, vmem_limit_bytes=60 * 1024 * 1024
        ),
    )(jnp.transpose(images[0], (1, 2, 0, 3)).reshape(PIX, N, C), targets, kernel, projection, captions)
    own = jnp.concatenate([kg[:, 0:PIX], kg[:, 64 : 64 + PIX]], axis=0)
    kernel_share = lax.dynamic_slice_in_dim(own, lax.axis_index("group") * 6, 6, 0)
    image_grad = jnp.transpose(image_grad.reshape(S, S, N, C), (2, 0, 1, 3))
    return loss[:, 0][None], image_grad[None], kernel_share


def solution(mesh):
    placed = (P("group", "loop", None, None, None), P("group", None), P(), P(), P("loop", None))
    return jax.shard_map(
        shards,
        mesh=mesh,
        in_specs=placed,
        out_specs=(
            P("group", "loop"),
            P("group", "loop", None, None, None),
            P(("loop", "group"), None),
        ),
        check_vma=False,
    )
```

```python
import jax
import jax.numpy as jnp
from jax import lax
from jax.experimental import pallas as pl
from jax.experimental.pallas import tpu as pltpu
from jax.sharding import PartitionSpec as P

MESH = pl.DeviceIdType.MESH
ORDER = (4, 5, 3, 6, 2, 7, 1, 0)
f32, bf16 = jnp.float32, jnp.bfloat16

SCALE = 20.0
EPS = 1e-06
C, D, S = 1536, 768, 7
T = C // 128
PIX = S * S
L, G = 32, 8
N = 8
H = L // 2
Q = L * N
CAPS = 4096
CH = 512
NCH = CAPS // CH


def remote(src, dst, send, recv, where):
    return pltpu.make_async_remote_copy(
        src_ref=src, dst_ref=dst, send_sem=send, recv_sem=recv, device_id=where, device_id_type=MESH
    )


PAIRS = ((4, 3), (2, 3), (6, 5), (4, 5), (2, 1), (0, 1))


def macs(acc, row, tap):
    for b in range(S):
        w = tap(b)
        for j in range(S):
            if 0 <= j + b - 3 < S:
                term = row[j + b - 3] * w
                acc[j] = term if acc[j] is None else acc[j] + term


def conv_rows(load, pair, tap, diff):
    def row(r):
        return [load(r, x) for x in range(S)]

    for o in range(4):
        both, low, high = [None] * S, [None] * S, [None] * S
        for q in range(4):
            d = q - o
            if abs(d) <= 1 and o < 3 and q < 3:
                a = 2 * d + 3
                macs(both, [pair(q, x) for x in range(S)], lambda b: tap(a, b))
                macs(low, row(2 * q + 1), lambda b: diff(a + 1, a, b))
                macs(high, row(2 * q), lambda b: diff(a - 1, a, b))
                continue
            for r in (2 * q, 2 * q + 1):
                for i, acc in ((2 * o, low), (2 * o + 1, high)):
                    if r < S and i < S and 0 <= r - i + 3 < S:
                        macs(acc, row(r), lambda b: tap(r - i + 3, b))
        for i, acc in ((2 * o, low), (2 * o + 1, high)):
            if i < S:
                yield i, [v if w is None else v + w for v, w in zip(acc, both)]


def mega(
    img_hbm, tgt_ref, ker_ref, proj_hbm, cap_hbm,
    loss_ref, ig_ref, kg_ref,
    img, proj, u, xf, kf, mub, nf, rsb, xs, kd, prs,
    qslots, qb, tcol, iot, cnt, e, irc, hit, pick, sgb, cols, cols2, rows,
    pacc, prec, rsend, rrec, dkr, kgt, kps, kprec, ksend, krec, krec2, kout,
    in_sem, ag_s, ag_r, fw_s, c1_s, c1_r, c2_s, c2_r, rw_s, rw_r,
    pp_s, pp_r, rs_s, rs_r, kp_s, kp_r, ks_s, ks_r, k2_s, k2_r,
):
    me = lax.axis_index("loop")
    grp = lax.axis_index("group")
    core, pos = me % 2, me // 2
    mate = {"loop": me + 1 - 2 * core}
    slot = core * H + pos

    def peer(p):
        return {"loop": p * 2 + core}

    c_img = pltpu.make_async_copy(img_hbm, img, in_sem.at[0])
    c_proj = pltpu.make_async_copy(proj_hbm, proj, in_sem.at[1])
    c_cap = pltpu.make_async_copy(cap_hbm, u, in_sem.at[2])
    c_img.start()
    c_proj.start()
    c_cap.start()
    barrier = pltpu.get_barrier_semaphore()

    def greet_loop(k, carry):
        pl.semaphore_signal(barrier, inc=1, device_id={"loop": lax.rem(me + k, L)}, device_id_type=MESH)
        return carry

    def greet_group(k, carry):
        pl.semaphore_signal(barrier, inc=1, device_id={"group": lax.rem(grp + k, G)}, device_id_type=MESH)
        return carry

    lax.fori_loop(1, L, greet_loop, 0)
    lax.fori_loop(1, G, greet_group, 0)

    def lanes(t):
        return pl.ds(pl.multiple_of(t * 128, 128), 128)

    c_img.wait()

    def tap_of(t, a, b):
        return jnp.broadcast_to(kf[t, a * 8 + b : a * 8 + b + 1, :], (N, 128))

    def diff_of(t, hi, lo, b):
        n = PAIRS.index((hi, lo)) * 8 + b
        return jnp.broadcast_to(kd[t, n : n + 1, :], (N, 128))

    def forward_tile(t, carry):
        for a in range(S):
            kf[t, a * 8 : a * 8 + S, :] = ker_ref[a, :, lanes(t)].astype(f32)
        total = None
        for p in range(PIX):
            v = img[p, :, lanes(t)].astype(f32)
            xf[t, p] = v
            total = v if total is None else total + v
        xs[t] = total
        for n, (hi, lo) in enumerate(PAIRS):
            kd[t, n * 8 : n * 8 + 8, :] = kf[t, hi * 8 : hi * 8 + 8, :] - kf[t, lo * 8 : lo * 8 + 8, :]
        for q in range(3):
            for x in range(S):
                prs[q * S + x] = xf[t, 2 * q * S + x] + xf[t, (2 * q + 1) * S + x]
        for i, acc in conv_rows(
            lambda r, x: xf[t, r * S + x],
            lambda q, x: prs[q * S + x],
            lambda a, b: tap_of(t, a, b),
            lambda hi, lo, b: diff_of(t, hi, lo, b),
        ):
            for j in range(S):
                nf[t, i * S + j] = acc[j]
        return carry

    lax.fori_loop(0, T, forward_tile, 0)

    def lane_mean(x):
        return jnp.broadcast_to(jnp.sum(x, axis=1, keepdims=True) * (1.0 / C), (N, 128))

    def mean_row(i, carry):
        for j in range(S):
            mub[i * S + j] = lane_mean(jnp.sum(nf[:, i * S + j], axis=0))
        return carry

    def var_row(i, carry):
        for j in range(S):
            p = i * S + j
            cen = nf[:, p] - mub[p][None]
            rsb[p] = lax.rsqrt(lane_mean(jnp.sum(cen * cen, axis=0)) + EPS)
        return carry

    def norm_row(i, acc):
        for j in range(S):
            p = i * S + j
            nrm = (nf[:, p] - mub[p][None]) * rsb[p][None]
            nf[:, p] = nrm
            acc = acc + nrm
        return acc

    lax.fori_loop(0, S, mean_row, 0)
    lax.fori_loop(0, S, var_row, 0)
    nsum = lax.fori_loop(0, S, norm_row, xs[...])
    pooled = (nsum * (1.0 / PIX)).astype(bf16)
    pooled = jnp.concatenate([pooled[t] for t in range(T)], axis=1)
    c_proj.wait()
    embedded = jnp.dot(pooled, proj[...], preferred_element_type=f32)
    inv_norm = lax.rsqrt(jnp.sum(embedded * embedded, axis=1, keepdims=True) + EPS)
    unit = embedded * inv_norm
    qslots[slot] = unit.astype(bf16)

    pl.semaphore_wait(barrier, L - 1 + G - 1)
    own_q = qslots.at[slot]

    def around(start):
        for k in range(H - 1):
            j = k + k // (H - 2)
            start(k, lax.rem(pos // 2 + ORDER[j // 2], 8) * 2 + lax.rem(pos % 2 + j % 2, 2))

    around(lambda k, to: remote(own_q, own_q, ag_s.at[k], ag_r.at[slot], peer(to)).start())
    remote(own_q, own_q, fw_s.at[0], ag_r.at[slot], mate).start()

    c_cap.wait()

    def unit_rows(r, carry):
        rng = pl.ds(pl.multiple_of(r * 128, 128), 128)
        v = u[rng, :].astype(f32)
        u[rng, :] = (v * lax.rsqrt(jnp.sum(v * v, axis=1, keepdims=True) + EPS)).astype(bf16)
        return carry

    lax.fori_loop(0, CAPS // 128, unit_rows, 0)
    local = (tgt_ref[...] - me * CAPS).astype(f32)
    for h in range(2):
        col = jnp.transpose(jnp.broadcast_to(local[:, h * 128 : h * 128 + 128], (128, 128)))
        for b in range(16):
            l = h * 16 + b
            s = (l % 2) * H + l // 2
            tcol[s * N : s * N + N, :] = col[b * N : b * N + N, :]
    iot[...] = lax.broadcasted_iota(jnp.int32, (N, CH), 1).astype(f32)

    def wide(x):
        return jnp.concatenate([x] * (CH // 128), axis=1)

    def hits(r, rng):
        ids = iot[0:1, :] + (r * float(CH) if isinstance(r, int) else (r * CH).astype(f32))
        return wide(tcol[rng, :]) == ids

    def count(r, carry):
        cnt[pl.ds(r, 1), :] = jnp.sum(jnp.where(hits(r, slice(None)), 1.0, 0.0), axis=0, keepdims=True)
        return carry


    def ag_forward(k, carry):
        frm = core * H + lax.rem(pos + k, H)
        got = qslots.at[frm]
        remote(got, got, ag_s.at[0], ag_r.at[frm], mate).wait_recv()
        remote(got, got, fw_s.at[k], ag_r.at[frm], mate).start()
        return carry

    lax.fori_loop(1, H, ag_forward, 0)

    def ag_mate(k, carry):
        frm = (1 - core) * H + k
        got = qslots.at[frm]
        remote(got, got, ag_s.at[0], ag_r.at[frm], mate).wait_recv()
        return carry

    lax.fori_loop(0, H, ag_mate, 0)

    def ag_done(k, carry):
        remote(own_q, own_q, ag_s.at[k], ag_r.at[0], mate).wait_send()
        return carry

    def fw_done(k, carry):
        remote(own_q, own_q, fw_s.at[k], ag_r.at[0], mate).wait_send()
        return carry

    qb[...] = qslots[...].astype(f32).reshape(Q, D).astype(bf16)

    def scores(r, carry):
        rng = pl.ds(pl.multiple_of(r * CH, CH), CH)
        s = lax.dot_general(qb[...], u[rng, :], (((1,), (1,)), ((), ())), preferred_element_type=f32)
        v = jnp.exp(SCALE * s)
        e[r] = v
        cols[grp, pl.ds(r, 1), :] = jnp.sum(v, axis=0, keepdims=True)
        return carry

    lax.fori_loop(0, NCH, scores, 0)
    lax.fori_loop(0, H - 1, ag_done, 0)
    lax.fori_loop(0, H, fw_done, 0)

    def group_exchange(buf, send, recv):
        own = buf.at[grp]

        def start(k, carry):
            remote(own, own, send.at[k], recv.at[grp], {"group": lax.rem(grp + k, G)}).start()
            return carry

        def arrive(k, carry):
            frm = lax.rem(grp + k, G)
            remote(own, buf.at[frm], send.at[k], recv.at[frm], {"group": frm}).wait()
            return carry

        lax.fori_loop(1, G, start, 0)
        return lambda: lax.fori_loop(1, G, arrive, 0)

    def picked(c, carry):
        rng = pl.ds(pl.multiple_of(c * 128, 128), 128)

        def chunk(r, carry):
            sgb[:, pl.ds(pl.multiple_of(r * CH, CH), CH)] = jnp.where(hits(r, rng), 1.0, 0.0).astype(bf16)
            return carry

        lax.fori_loop(0, NCH, chunk, 0)
        pick[c] = jnp.dot(sgb[...], u[...], preferred_element_type=f32)
        return carry

    finish = group_exchange(cols, c1_s, c1_r)
    lax.fori_loop(0, NCH, count, 0)
    lax.fori_loop(0, 2, picked, 0)
    finish()
    ic = 1.0 / jnp.sum(cols[...], axis=0)
    cols[0] = ic

    def row_pass(q, carry):
        rng = pl.ds(pl.multiple_of(q * 32, 32), 32)
        acc = None
        for r in range(NCH):
            w = e[r, rng, :] * cols[0, r : r + 1, :]
            for b in range(CH // 128):
                v = w[:, b * 128 : b * 128 + 128]
                acc = v if acc is None else acc + v
        irc[rng, :] = acc
        return carry

    lax.fori_loop(0, Q // 32, row_pass, 0)
    rows[me] = jnp.concatenate(
        [jnp.sum(jnp.transpose(irc[h * 128 : h * 128 + 128, :]), axis=0, keepdims=True) for h in range(2)], axis=0
    )
    own_r = rows.at[me]

    for k in range(L):
        zo, low = ORDER[k // 4], k % 4
        if zo == 0 and low == 0:
            continue
        to = (lax.rem(pos // 2 + zo, 8) * 2 + lax.rem(pos % 2 + low // 2, 2)) * 2 + lax.rem(core + low % 2, 2)
        remote(own_r, own_r, rw_s.at[k], rw_r.at[me], {"loop": to}).start()

    def hit_pass(q, carry):
        rng = pl.ds(pl.multiple_of(q * 32, 32), 32)
        acc = None
        for r in range(NCH):
            z = jnp.where(hits(r, rng), e[r, rng, :] * cols[0, r : r + 1, :], 0.0)
            for b in range(CH // 128):
                v = z[:, b * 128 : b * 128 + 128]
                acc = v if acc is None else acc + v
        hit[rng, :] = acc
        return carry

    lax.fori_loop(0, Q // 32, hit_pass, 0)

    def row_wait(k, carry):
        frm = lax.rem(me + k, L)
        remote(own_r, rows.at[frm], rw_s.at[0], rw_r.at[frm], {"loop": frm}).wait_recv()
        return carry

    def row_sent(k, carry):
        remote(own_r, own_r, rw_s.at[k], rw_r.at[0], mate).wait_send()
        return carry

    lax.fori_loop(1, L, row_wait, 0)
    tot = jnp.sum(rows[...], axis=0)

    def spread(x):
        return jnp.transpose(jnp.broadcast_to(x, (128, 128)))

    inv = 1.0 / tot
    for h in range(2):
        irc[h * 128 : h * 128 + 128, :] = spread(inv[h : h + 1])

    def grad_pass(r, carry):
        y = e[r] * wide(irc[...])
        cols2[grp, pl.ds(r, 1), :] = (
            jnp.sum(y, axis=0, keepdims=True) * cols[0, pl.ds(r, 1), :] - cnt[pl.ds(r, 1), :]
        )
        return carry

    lax.fori_loop(0, NCH, grad_pass, 0)
    finish = group_exchange(cols2, c2_s, c2_r)
    for k in range(L):
        if k != ORDER.index(0) * 4:
            row_sent(k, 0)
    finish()
    cols2[0] = jnp.sum(cols2[...], axis=0)

    def half_grad(c):
        rng = pl.ds(pl.multiple_of(c * 128, 128), 128)

        def chunk(r, carry):
            base = wide(irc[rng, :]) - cols2[0, pl.ds(r, 1), :]
            g = e[r, rng, :] * (cols[0, pl.ds(r, 1), :] * base)
            sgb[:, pl.ds(pl.multiple_of(r * CH, CH), CH)] = g.astype(bf16)
            return carry

        lax.fori_loop(0, NCH, chunk, 0)
        return SCALE * (jnp.dot(sgb[...], u[...], preferred_element_type=f32) - pick[c])

    def with_hits(c):
        part = hit[pl.ds(pl.multiple_of(c * 128, 128), 128), :]
        return jnp.concatenate([half_grad(c), part], axis=1).reshape(H, N, D + 128)

    pacc[...] = with_hits(1 - core)
    to_mate = remote(pacc, prec, pp_s, pp_r, mate)
    to_mate.start()
    mine = with_hits(core)
    to_mate.wait()
    both = (mine + prec[...]).reshape(H * N, D + 128)
    found = jnp.broadcast_to(jnp.sum(both[:, D:], axis=1, keepdims=True), (H * N, 128))
    first = found.astype(bf16).astype(f32)
    second = (found - first).astype(bf16).astype(f32)
    lane = lax.broadcasted_iota(jnp.int32, (H * N, 128), 1)
    found = jnp.where(lane == 0, first, jnp.where(lane == 1, second, jnp.where(lane == 2, found - first - second, 0.0)))
    both = jnp.concatenate([both[:, 0:D], found], axis=1).reshape(H, N, D + 128)
    rsend[...] = both.astype(bf16)

    def scatter_start(src, dst, send, recv):
        around(lambda k, to: remote(src.at[to], dst.at[pos], send.at[k], recv.at[pos], peer(to)).start())

    def scatter_wait(src, dst, send, recv):
        def arrive(k, carry):
            frm = lax.rem(pos + k, H)
            remote(src.at[frm], dst.at[frm], send.at[k - 1], recv.at[frm], peer(frm)).wait()
            return carry

        lax.fori_loop(1, H, arrive, 0)

    rrec[pos] = rsend[pos]
    scatter_start(rsend, rrec, rs_s, rs_r)
    scatter_wait(rsend, rrec, rs_s, rs_r)
    qh = jnp.sum(rrec[...].astype(f32), axis=0)
    qg = qh[:, 0:D]
    own_rows = irc[pl.ds(pl.multiple_of(slot * N, N), N), :]
    los = -jnp.log(own_rows) - jnp.log(jnp.sum(qh[:, D:], axis=1, keepdims=True))
    eye = lax.broadcasted_iota(jnp.int32, (N, 128), 0) == lax.broadcasted_iota(jnp.int32, (N, 128), 1)
    loss_ref[...] = jnp.sum(jnp.where(eye, los, 0.0), axis=0, keepdims=True)[:, 0:N]

    eg = ((qg - unit * jnp.sum(unit * qg, axis=1, keepdims=True)) * inv_norm).astype(bf16)
    pg = lax.dot_general(eg, proj[...], (((1,), (1,)), ((), ())), preferred_element_type=f32)
    og = pg * (1.0 / PIX)
    centred = og - jnp.sum(og, axis=1, keepdims=True) * (1.0 / C)
    for t in range(T):
        xs[t] = og[:, t * 128 : t * 128 + 128]
        dkr[t, 0:N, :] = centred[:, t * 128 : t * 128 + 128]

    def hidden_row(i, carry):
        for j in range(S):
            p = i * S + j
            nrm = nf[:, p]
            m2 = jnp.sum(jnp.sum(nrm * xs[...], axis=0), axis=1, keepdims=True) * (1.0 / C)
            nf[:, p] = rsb[p][None] * (dkr[:, 0:N, :] - nrm * m2[None])
        return carry

    lax.fori_loop(0, S, hidden_row, 0)

    def kernel_tile(t, carry):
        dkr[t, 48:64, :] = jnp.zeros((16, 128), f32)
        def corr(acc, x, g):
            for b in range(S):
                for j in range(S):
                    if 0 <= j + b - 3 < S:
                        term = x[j + b - 3] * g[j]
                        acc[b] = term if acc[b] is None else acc[b] + term

        def line(ref, r):
            return [ref[t, r * S + c] for c in range(S)]

        def fold(a, acc, first):
            for b in range(S):
                v = jnp.sum(acc[b], axis=0, keepdims=True)
                at = slice(a * S + b, a * S + b + 1)
                dkr[t, at, :] = v if first else dkr[t, at, :] + v

        for a in range(S):
            acc = [None] * S
            for i in range(S):
                r = i + a - 3
                if 0 <= r < S and (r // 2 == 3 or i // 2 == 3 or abs(r // 2 - i // 2) > 1):
                    corr(acc, line(xf, r), line(nf, i))
            if acc[0] is None:
                dkr[t, a * S : a * S + S, :] = jnp.zeros((S, 128), f32)
            else:
                fold(a, acc, True)
        for d in (-1, 0, 1):
            both, low, high = [None] * S, [None] * S, [None] * S
            for o in range(3):
                q = o + d
                if not 0 <= q < 3:
                    continue
                x0, x1, g0, g1 = line(xf, 2 * q), line(xf, 2 * q + 1), line(nf, 2 * o), line(nf, 2 * o + 1)
                corr(low, x1, g0)
                corr(high, x0, g1)
                corr(both, [u0 + u1 for u0, u1 in zip(x0, x1)], [u0 + u1 for u0, u1 in zip(g0, g1)])
            fold(2 * d + 3, [v - (l0 + h0) for v, l0, h0 in zip(both, low, high)], False)
            fold(2 * d + 4, low, False)
            fold(2 * d + 2, high, False)
        flat = jnp.concatenate([dkr[t], jnp.zeros((64, 128), f32)], axis=0)
        kgt[lanes(t), :] = jnp.transpose(flat)
        return carry

    lax.fori_loop(0, T, kernel_tile, 0)

    def pack(l, carry):
        c = l % 2
        low = kgt[pl.ds(pl.multiple_of(l * 48, 8), 24), :]
        high = kgt[pl.ds(pl.multiple_of(l * 48 + 24, 8), 24), :]
        kps[c * H + l // 2] = low + pltpu.roll(high, 64, 1)
        return carry

    lax.fori_loop(0, L, pack, 0)
    other = pl.ds((1 - core) * H, H)
    k_mate = remote(kps.at[other], kprec, kp_s, kp_r, mate)
    k_mate.start()

    def image_tile(t, carry):
        for q in range(3):
            for x in range(S):
                prs[q * S + x] = nf[t, 2 * q * S + x] + nf[t, (2 * q + 1) * S + x]
        for i, acc in conv_rows(
            lambda r, x: nf[t, r * S + x],
            lambda q, x: prs[q * S + x],
            lambda a, b: tap_of(t, S - 1 - a, S - 1 - b),
            lambda hi, lo, b: diff_of(t, S - 1 - hi, S - 1 - lo, S - 1 - b),
        ):
            for j in range(S):
                ig_ref[i * S + j, :, lanes(t)] = (acc[j] + xs[t]).astype(bf16)
        return carry

    lax.fori_loop(0, 3, image_tile, 0)
    k_mate.wait()
    ksum = kps.at[pl.ds(core * H, H)]
    ksend[...] = (kprec[...] + ksum[...]).astype(bf16)
    krec[pos] = ksend[pos]
    scatter_start(ksend, krec, ks_s, ks_r)
    lax.fori_loop(3, 9, image_tile, 0)
    scatter_wait(ksend, krec, ks_s, ks_r)
    krec2[grp] = jnp.sum(krec[...].astype(f32), axis=0)
    finish = group_exchange(krec2, k2_s, k2_r)
    lax.fori_loop(9, T, image_tile, 0)
    finish()
    kout[24:32, :] = jnp.zeros((8, 128), f32)
    kout[0:24, :] = jnp.sum(krec2[...], axis=0)
    quarter = kout[pl.ds(lax.rem(grp, 4) * 6, 8), :]
    kg_ref[...] = pltpu.roll(quarter, lax.div(grp, 4) * 64, 1)[0:6, 0:PIX]


def shards(images, targets, kernel, projection, captions):
    vmem = pltpu.VMEM
    dma = pltpu.SemaphoreType.DMA
    anyspace = pl.BlockSpec(memory_space=pl.ANY)
    whole = pl.BlockSpec(memory_space=vmem)
    scratch = [
        vmem((PIX, N, C), bf16),
        vmem((C, D), bf16),
        vmem((CAPS, D), bf16),
        vmem((T, PIX, N, 128), f32),
        vmem((T, 56, 128), f32),
        vmem((PIX, N, 128), f32),
        vmem((T, PIX, N, 128), f32),
        vmem((PIX, N, 128), f32),
        vmem((T, N, 128), f32),
        vmem((T, 48, 128), f32),
        vmem((21, N, 128), f32),
        vmem((L, N, D), bf16),
        vmem((Q, D), bf16),
        vmem((Q, 128), f32),
        vmem((N, CH), f32),
        vmem((NCH, CH), f32),
        vmem((NCH, Q, CH), f32),
        vmem((Q, 128), f32),
        vmem((Q, 128), f32),
        vmem((2, Q // 2, D), f32),
        vmem((Q // 2, CAPS), bf16),
        vmem((G, NCH, CH), f32),
        vmem((G, NCH, CH), f32),
        vmem((L, 2, 128), f32),
        vmem((H, N, D + 128), f32),
        vmem((H, N, D + 128), f32),
        vmem((H, N, D + 128), bf16),
        vmem((H, N, D + 128), bf16),
        vmem((T, 64, 128), f32),
        vmem((C, 128), f32),
        vmem((L, 24, 128), f32),
        vmem((H, 24, 128), f32),
        vmem((H, 24, 128), bf16),
        vmem((H, 24, 128), bf16),
        vmem((G, 24, 128), f32),
        vmem((32, 128), f32),
        dma((3,)), dma((H,)), dma((L,)), dma((H,)),
        dma((G,)), dma((G,)), dma((G,)), dma((G,)),
        dma((L,)), dma((L,)),
        dma, dma, dma((H,)), dma((H,)),
        dma, dma, dma((H,)), dma((H,)), dma((G,)), dma((G,)),
    ]
    loss, image_grad, kg = pl.pallas_call(
        mega,
        name="mega",
        out_shape=(
            jax.ShapeDtypeStruct((1, N), f32),
            jax.ShapeDtypeStruct((PIX, N, C), bf16),
            jax.ShapeDtypeStruct((6, PIX), f32),
        ),
        in_specs=[anyspace, whole, whole, anyspace, anyspace],
        out_specs=(whole, whole, whole),
        scratch_shapes=scratch,
        compiler_params=pltpu.CompilerParams(
            collective_id=0, has_side_effects=True, vmem_limit_bytes=60 * 1024 * 1024
        ),
    )(jnp.transpose(images[0], (1, 2, 0, 3)).reshape(PIX, N, C), targets, kernel, projection, captions)
    image_grad = jnp.transpose(image_grad.reshape(S, S, N, C), (2, 0, 1, 3))
    return loss, image_grad[None], kg


def solution(mesh):
    placed = (P("group", "loop", None, None, None), P("group", None), P(), P(), P("loop", None))
    return jax.shard_map(
        shards,
        mesh=mesh,
        in_specs=placed,
        out_specs=(
            P("group", "loop"),
            P("group", "loop", None, None, None),
            P(("loop", "group"), None),
        ),
        check_vma=False,
    )
```
